32 devices in a mesh: section: 4 (over y, core), expert: 8 (over z, x).
Axes of the slice: x: 2, y: 2, z: 4, core: 2. Of those that a mesh axis runs over, the one named last changes fastest.
Arguments:
- activations: bfloat16 [2048, 6144], P('expert', 'section'), may hold values from -6 to 6
- router_weight: bfloat16 [8, 6144], P(None, 'section'), may hold values from -0.078125 to 0.078125
- w_up: bfloat16 [65536, 6144], P('expert', 'section'), may hold values from -0.078125 to 0.078125
- w_down: bfloat16 [65536, 6144], P('expert', 'section'), may hold values from -0.0625 to 0.0625
- expert_ids: int32 [2048, 2], P('expert'), may hold values from 0 to 7, all different within a row; in each aligned block of 256 rows (0 to 255, 256 to 511, ...) at most 64 rows name the same one
Outputs:
- layer_out: bfloat16 [2048, 6144], P('expert', 'section')
The draws below stay inside these ranges and needn't reach their ends.
Inputs may be any that keep to these rules, and one draw needn't show every extreme that they name: `expert_ids`: among the 256 tokens of one device (one aligned block of rows) each expert is named exactly 64 times; the two ids of a token differ.
All inputs are finite; a program needn't handle non-finite values.
Results may differ from the reference program's by a relative error of at most 0.009.
Values may be sent and summed in bfloat16 or wider, within the bound.
No kernel may reach another device: no remote copies, remote signals or barrier semaphores. Data moves between devices by JAX's collectives and lax.ppermute only.
A program may use at most 192 MiB of HBM per device.

```python
import math
import jax
import jax.numpy as jnp
import numpy as np
from jax import lax

D = 6144
HID = 8192
EXPERTS = 8
TOK_DEV = 256
QUARTERS = 1
CAP = 64
TOKENS = 2048
N_SECTION = 4
N_EXPERT = 8


def shard_levels(rng, dims, split, smallest, top_value):
    def one(dim, blocks):
        draws = jax.random.uniform(jax.random.fold_in(jax.random.fold_in(rng, 6), dim), (blocks,), jnp.float32, smallest / len(split), top_value / len(split))
        return jnp.repeat(jnp.exp(draws), dims[dim] // blocks).reshape((-1,) + (1,) * (len(dims) - dim - 1))

    gain = one(*split[0])
    for cut in split[1:]:
        gain = gain * one(*cut)
    return gain


def assign_block(rng, own, number, rows, number_of, top, most, lean):
    ranking = jax.random.permutation(rng, number_of)
    packed, usual = portions_of(number_of, rows * top, most, lean, True), portions_of(number_of, rows * top, most, lean, False)
    places = jnp.arange(number_of)

    def named(sizes, turn):
        used = int((sizes > 0).sum())
        fixed = max(1, used // 4)
        moved = fixed + (places - fixed + turn * (used - fixed)) % max(1, number_of - fixed)
        return jnp.zeros((number_of,), jnp.int32).at[ranking[jnp.where(places < fixed, places, moved)]].set(jnp.asarray(sizes, jnp.int32))

    sizes = jnp.where(number % 4 == 0, named(packed, number // 4), named(usual, number - number // 4 - 1))
    mixed = jax.random.permutation(jax.random.fold_in(own, 3), number_of)
    giver, receiver = mixed[0:number_of // 2 * 2:2], mixed[1:number_of // 2 * 2:2]
    slack = jnp.minimum(sizes[giver] - 1, most - sizes[receiver]) // 2
    slack = jnp.where((giver == ranking[0]) | (receiver == ranking[0]) | (sizes[receiver] == 0), 0, jnp.maximum(slack, 0))
    moved = jax.random.randint(jax.random.fold_in(own, 4), (number_of // 2,), 0, 1 << 20) % (slack + 1)
    sizes = sizes.at[giver].add(-moved).at[receiver].add(moved)
    members = jnp.searchsorted(jnp.cumsum(sizes), jnp.arange(rows * top), side="right").astype(jnp.int32)
    grid = members.reshape(top, rows).T
    grid = grid[jax.random.permutation(jax.random.fold_in(own, 1), rows)]
    turn = jax.random.randint(jax.random.fold_in(own, 2), (rows, 1), 0, top)
    return jnp.take_along_axis(grid, (jnp.arange(top)[None, :] + turn) % top, axis=1)


def portions_of(amount, total, most, lean, full):
    portions = [(1 << 20) // math.isqrt(rank ** lean) + 1 for rank in range(1, amount + 1)]
    largest = most if full else min(most, max(-(-total // amount), total * portions[0] // sum(portions)))
    least = 1 if total - largest >= amount - 1 else 0
    given, surplus = [largest] + [least] * (amount - 1), total - largest - least * (amount - 1)
    while surplus > 0:
        movable = [i for i in range(1, amount) if given[i] < largest] or [i for i in range(1, amount) if given[i] < most]
        whole, budget = sum([portions[i] for i in movable]), surplus
        for i in movable:
            extra = min(most - given[i], max(1, budget * portions[i] // whole), surplus)
            given[i] = given[i] + extra
            surplus = surplus - extra
    return np.array(given)


def normal_values(own_key, shape, scale, reach, split=(), kind=jnp.bfloat16):
    result = jax.random.normal(own_key, shape, jnp.float32) * scale
    if len(split) > 0:
        result = shard_levels(own_key, shape, split, -0.22, 0.18) * result
    return jnp.clip(result, min=-reach, max=reach).astype(kind)


def setup_inputs(seed: int = 0) -> dict:
    splits = jax.random.split(jax.random.key(seed), 6)
    activations = normal_values(splits[0], (TOKENS, D), 1.0, 6.0, ((0, 8), (1, 4)))
    router_weight = normal_values(splits[1], (EXPERTS, D), D ** -0.5, 0.078125, ((1, 4),))
    w_up = normal_values(splits[2], (EXPERTS * HID, D), D ** -0.5, 0.078125, ((0, 8), (1, 4)))
    w_down = normal_values(splits[3], (EXPERTS * HID, D), HID ** -0.5, 0.0625, ((0, 8), (1, 4)))
    expert_ids_keys = jax.random.split(jax.random.fold_in(splits[4], 1), TOKENS // TOK_DEV)
    expert_ids_turns = jax.random.permutation(jax.random.fold_in(splits[4], 3), TOKENS // TOK_DEV)
    expert_ids = jax.vmap(lambda own, number: assign_block(jax.random.fold_in(splits[4], 2), own, number, TOK_DEV, EXPERTS, 2, CAP, 0))(expert_ids_keys, expert_ids_turns).reshape((TOKENS, 2))
    return {"activations": activations, "router_weight": router_weight, "w_up": w_up, "w_down": w_down, "expert_ids": expert_ids}


def reference(activations, router_weight, w_up, w_down, expert_ids):
    logits = jnp.dot(activations, router_weight.T, preferred_element_type=jnp.float32)
    chosen = jnp.take_along_axis(logits, expert_ids, axis=1)
    gates = jax.nn.sigmoid(chosen - chosen[:, ::-1])
    ids_blocks = expert_ids.reshape(N_EXPERT, TOK_DEV * 2)
    onehot = (ids_blocks[:, :, None] == jnp.arange(EXPERTS, dtype=jnp.int32)[None, None, :]).astype(jnp.int32)
    rank_in = jnp.sum((jnp.cumsum(onehot, axis=1) - onehot) * onehot, axis=2).astype(jnp.int32)
    slots = (ids_blocks * CAP + rank_in).astype(jnp.int32)

    def fill_block(block_rows, block_slots):
        empty = jnp.zeros((EXPERTS * CAP, D), jnp.bfloat16)
        return empty.at[block_slots].set(jnp.repeat(block_rows, 2, axis=0))

    buffers = jax.vmap(fill_block)(activations.reshape(N_EXPERT, TOK_DEV, D), slots)
    buffers = buffers.reshape(N_EXPERT, EXPERTS, CAP, D).transpose(1, 0, 2, 3).reshape(EXPERTS, N_EXPERT * CAP, D)
    up_all = w_up.reshape(EXPERTS, HID, D)
    down_all = w_down.reshape(EXPERTS, HID, D)
    cols = D // N_SECTION
    units = HID // QUARTERS

    def run_expert(operands):
        rows, up_rows, down_rows = operands
        pre = jnp.zeros((rows.shape[0], HID), jnp.float32)
        for block in range(N_SECTION):
            part = jnp.dot(rows[:, block * cols:(block + 1) * cols], up_rows[:, block * cols:(block + 1) * cols].T, preferred_element_type=jnp.float32)
            pre = pre + lax.optimization_barrier(part.astype(jnp.bfloat16)).astype(jnp.float32)
        hidden = jax.nn.silu(pre).astype(jnp.bfloat16)
        total = jnp.zeros((rows.shape[0], D), jnp.float32)
        for block in range(QUARTERS):
            part = jnp.dot(hidden[:, block * units:(block + 1) * units], down_rows[block * units:(block + 1) * units], preferred_element_type=jnp.float32)
            total = total + lax.optimization_barrier(part.astype(jnp.bfloat16)).astype(jnp.float32)
        return total

    expert_out = lax.map(run_expert, (buffers, up_all, down_all))
    flat_out = expert_out.reshape(EXPERTS * N_EXPERT * CAP, D)
    block_index = jnp.arange(N_EXPERT, dtype=jnp.int32)[:, None]
    where = (ids_blocks * (N_EXPERT * CAP) + block_index * CAP + rank_in).reshape(-1).astype(jnp.int32)
    picked = flat_out[where].reshape(TOKENS, 2, D)
    mixed = activations.astype(jnp.float32) + jnp.sum(gates[:, :, None] * picked, axis=1)
    return mixed.astype(jnp.bfloat16)
```

```python
import functools

import jax
import jax.numpy as jnp
from jax import lax
from jax.experimental import pallas as pl
from jax.experimental.pallas import tpu as pltpu
from jax.sharding import PartitionSpec as P

BF = jnp.bfloat16
F32 = jnp.float32
VM = pl.BlockSpec(memory_space=pltpu.VMEM)
ANY = pl.BlockSpec(memory_space=pl.ANY)
HBM = pl.BlockSpec(memory_space=pltpu.HBM)
LONG = pl.CostEstimate(flops=10**12, bytes_accessed=1, transcendentals=0)
COST = pl.CostEstimate(flops=1, bytes_accessed=1, transcendentals=0)
SM = pl.BlockSpec(memory_space=pltpu.SMEM)
TILE = 512
SLOTS = 4
NP = 4
LIMIT = 40


def kernel_call(kernel, **options):
    return pl.pallas_call(kernel, **{"cost_estimate": COST, **options})


def sds(shape, dtype=BF):
    return jax.ShapeDtypeStruct(shape, dtype)


def params(mib):
    return pltpu.CompilerParams(vmem_limit_bytes=mib << 20)


def plain(activations, router_weight, w_up, w_down, expert_ids):
    group = lax.axis_size("expert")
    experts = router_weight.shape[0]
    quarters = group // experts
    tok_rows, columns = activations.shape
    capacity = tok_rows // 4
    total_rows = experts * capacity
    logits = lax.psum(
        lax.dot_general(
            activations, router_weight, (((1,), (1,)), ((), ())), preferred_element_type=F32
        ),
        "section",
    )
    selected = expert_ids[:, :, None] == jnp.arange(experts, dtype=jnp.int32)[None, None, :]
    chosen = jnp.sum(jnp.where(selected, logits[:, None, :], 0.0), axis=2)
    gates = jax.nn.sigmoid(chosen - chosen[:, ::-1])
    flat_ids = expert_ids.reshape(-1)
    onehot = flat_ids[:, None] == jnp.arange(experts, dtype=jnp.int32)[None, :]
    places = jnp.arange(flat_ids.shape[0])
    before = (places[None, :] < places[:, None]).astype(BF)
    counts = jnp.dot(before, onehot.astype(BF), preferred_element_type=F32)
    rank_in = jnp.sum(jnp.where(onehot, counts, 0.0), axis=1).astype(jnp.int32)
    targets = flat_ids * capacity + rank_in
    outgoing = (
        jnp.zeros((total_rows, columns), BF).at[targets].set(jnp.repeat(activations, 2, axis=0))
    )
    outgoing = jnp.repeat(outgoing.reshape(experts, capacity, columns), quarters, axis=0)
    received = lax.all_to_all(outgoing, "expert", split_axis=0, concat_axis=0, tiled=True)
    senders, items = received.shape[:2]
    rows = received.reshape(senders * items, columns)
    pre_part = lax.dot_general(rows, w_up, (((1,), (1,)), ((), ())), preferred_element_type=F32)
    whole = lax.psum(pre_part.astype(BF), "section").astype(F32)
    hidden = jax.nn.silu(whole).astype(BF)
    result = jnp.dot(hidden, w_down, preferred_element_type=F32)
    result = result.astype(BF).reshape(senders, items, columns)
    returned = lax.all_to_all(result, "expert", split_axis=0, concat_axis=0, tiled=True)
    returned = (
        returned.reshape(experts, quarters, capacity, columns)
        .transpose(1, 0, 2, 3)
        .reshape(quarters, total_rows, columns)
    )
    onehot = (targets[:, None] == jnp.arange(total_rows)[None, :]).astype(BF)
    picked = jnp.einsum("ts,qsd->td", onehot, returned, preferred_element_type=F32)
    picked = picked.reshape(tok_rows, 2, columns)
    mixed = activations.astype(F32) + jnp.sum(gates[:, :, None] * picked, axis=1)
    return mixed.astype(BF)


PARTS = 8


def cut_copies(first, core, half, w_ref, o_ref, hold, sem):
    step = o_ref.shape[0] // PARTS
    start = pl.multiple_of((1 - core) * half + first, step)
    ins = [
        pltpu.make_async_copy(w_ref.at[pl.ds(start + i * step, step), :], hold.at[i], sem.at[i])
        for i in range(PARTS)
    ]
    outs = [
        pltpu.make_async_copy(hold.at[i], o_ref.at[pl.ds(i * step, step), :], sem.at[PARTS + i])
        for i in range(PARTS)
    ]
    return ins, outs


def pack_kernel(cap, peers, me_ref, a_ref, t_ref, *outs):
    low = me_ref[0]
    per = len(peers) // len(outs)
    for i, j in enumerate(peers):
        at = i % per * cap
        outs[i // per][at : at + cap, :] = a_ref[low ^ j]


def cut_kernel(first, half, me_ref, w_ref, t_ref, o_ref, hold, sem):
    ins, outs = cut_copies(first, me_ref[0], half, w_ref, o_ref, hold, sem)
    for c in ins:
        c.start()
    for i, o in zip(ins, outs):
        i.wait()
        o.start()
    for o in outs:
        o.wait()


def cut_scratch(rows, columns):
    return [
        pltpu.VMEM((PARTS, rows // PARTS, columns), BF),
        pltpu.SemaphoreType.DMA((2 * PARTS,)),
    ]


def route_kernel(cap, me_ref, ids_ref, act_ref, router_ref, *outs):
    slot_ref, logit_ref, near_ref, all_ref = outs
    experts = router_ref.shape[0]
    tokens = act_ref.shape[0]
    low = me_ref[0] & 3
    ids = ids_ref[...] ^ me_ref[0]
    id0, id1 = ids[0:1, :], ids[1:2, :]
    line = lax.broadcasted_iota(jnp.int32, (experts, tokens), 0)
    is0, is1 = line == id0, line == id1
    member = (is0 | is1).astype(F32).astype(BF)
    r = lax.broadcasted_iota(jnp.int32, (tokens, tokens), 0)
    c = lax.broadcasted_iota(jnp.int32, (tokens, tokens), 1)
    rank = jnp.dot(member, (r < c).astype(F32).astype(BF), preferred_element_type=F32)
    first = line.astype(F32) * cap + rank
    slot0 = jnp.sum(jnp.where(is0, first, 0.0), axis=0, keepdims=True)
    slot1 = jnp.sum(jnp.where(is1, first, 0.0), axis=0, keepdims=True)
    slot_ref[...] = jnp.concatenate([slot0, slot1] + [jnp.zeros_like(slot0)] * 6, axis=0)
    act = act_ref[...]
    i0, i1 = slot0.astype(jnp.int32), slot1.astype(jnp.int32)
    s = lax.broadcasted_iota(jnp.int32, (experts * cap, tokens), 0)
    pick = ((s == i0) | (s == i1)).astype(F32).astype(BF)
    for j in range(experts):
        rows = jnp.dot(pick[j * cap : (j + 1) * cap], act, preferred_element_type=F32).astype(BF)
        if j < 4:
            near_ref[low ^ j] = rows
        all_ref[me_ref[0] ^ j] = rows
    logit_ref[...] = lax.dot_general(
        router_ref[...], act, (((1,), (1,)), ((), ())), preferred_element_type=F32
    )


def silu_kernel(a_ref, b_ref, t_ref, o_ref):
    v = a_ref[...].astype(F32) + b_ref[...].astype(F32)
    o_ref[...] = (v / (1.0 + jnp.exp(-v))).astype(BF)


def stream(sources, count, use):
    slots = min(SLOTS, count)

    def copies(g):
        for locate, buf, sem in sources:
            ref, row = locate(g)
            yield pltpu.make_async_copy(
                ref.at[pl.ds(pl.multiple_of(row, TILE), TILE), :],
                buf.at[g % slots],
                sem.at[g % slots],
            )

    for g in range(slots):
        for c in copies(g):
            c.start()
    for g in range(count):
        for c in copies(g):
            c.wait()
        use(g, *[buf.at[g % slots] for _, buf, _ in sources])
        if g + slots < count:
            for c in copies(g + slots):
                c.start()


def up_kernel(half, span, pieces, n_x, corners, me_ref, *refs):
    mine_refs, their_refs = refs[:n_x], refs[n_x : 2 * n_x]
    w_ref, *got_refs = refs[2 * n_x : 2 * n_x + 3]
    n_p = len(pieces)
    x, y, buf_a, sem_a, buf_b, sem_b = refs[-6:]
    core = me_ref[0]
    out_refs = refs[-6 - len(corners) : -6]
    rows = mine_refs[0].shape[0]
    for i in range(n_x):
        x[i * rows : (i + 1) * rows, :] = mine_refs[i][...]
        y[i * rows : (i + 1) * rows, :] = their_refs[i][1 - core]
    each = span // TILE

    def locate_a(g):
        return w_ref, core * half + pieces[g // each] * span + (g % each) * TILE

    def locate_b(g):
        row = pieces[g // each] * span + (g % each) * TILE
        return got_refs[row // (half // 2)], row % (half // 2)

    dims = (((1,), (1,)), ((), ()))

    def use(g, a, b):
        v = (
            lax.dot_general(x[...], a[...], dims, preferred_element_type=F32)
            + lax.dot_general(y[...], b[...], dims, preferred_element_type=F32)
        ).astype(BF)
        for o, (row, col) in zip(out_refs, corners):
            at = g * TILE - col
            if 0 <= at < o.shape[1]:
                o[:, at : at + TILE] = v[row : row + o.shape[0], :]

    stream([(locate_a, buf_a, sem_a), (locate_b, buf_b, sem_b)], each * n_p, use)


def down_kernel(half, plan, ready, has_acc, me_ref, *refs):
    n_in = plan[-1][1] + 1
    wide = 1 if ready else 2
    s_refs = refs[: wide * n_in]
    w_ref, got_ref = refs[wide * n_in : wide * n_in + 2]
    k = wide * n_in + 2
    acc_refs = refs[k : k + 2] if has_acc else None
    k += 1 + (2 if has_acc else 0)
    own_ref, *oth_refs = refs[k:-7]
    h, own, oth, buf_a, sem_a, buf_b, sem_b = refs[-7:]
    core = me_ref[0]

    def locate_a(g):
        return w_ref, core * half + plan[g][0]

    def locate_b(g):
        return got_ref, plan[g][0]

    def use(g, a, b):
        _, i, c = plan[g]
        cols = slice(c, c + TILE)
        if ready:
            h[...] = s_refs[i][:, cols]
        else:
            v = s_refs[2 * i][:, cols].astype(F32) + s_refs[2 * i + 1][:, cols].astype(F32)
            h[...] = (v / (1.0 + jnp.exp(-v))).astype(BF)
        for i, (total, w) in enumerate(((own, a), (oth, b))):
            part = jnp.dot(h[...], w[...], preferred_element_type=F32)
            if g == 0:
                total[...] = part + acc_refs[i][...] if has_acc else part
            else:
                total[...] += part

    stream([(locate_a, buf_a, sem_a), (locate_b, buf_b, sem_b)], len(plan), use)
    own_ref[...] = own[...]
    each = own.shape[0] // len(oth_refs)
    for i, r in enumerate(oth_refs):
        r[...] = oth[i * each : (i + 1) * each, :].astype(r.dtype)


def finish_kernel(cap, near, parts, me_ref, own_ref, *refs):
    got_refs, outs = refs[:parts], refs[parts + 1 :]
    core, low = me_ref[0], me_ref[1]
    got = jnp.concatenate([r[1 - core] for r in got_refs], axis=0)
    for i in range(own_ref.shape[0] // cap):
        rows = slice(i * cap, (i + 1) * cap)
        v = (own_ref[rows, :] + got[rows, :].astype(F32)).astype(BF)
        if near:
            outs[0][low ^ i] = v
        else:
            outs[i][...] = v


def combine_kernel(cap, peers, me_ref, ids_ref, slot_ref, logit_ref, acc_ref, *refs):
    n = 1 if peers is None else len(peers)
    r_refs = refs[:n]
    out_ref = refs[n + 1]
    experts, tokens = logit_ref.shape
    line = lax.broadcasted_iota(jnp.int32, (experts, tokens), 0)
    ids = ids_ref[...]
    logits = logit_ref[...]
    c0 = jnp.sum(jnp.where(line == ids[0:1, :], logits, 0.0), axis=0, keepdims=True)
    c1 = jnp.sum(jnp.where(line == ids[1:2, :], logits, 0.0), axis=0, keepdims=True)
    g0, g1 = jax.nn.sigmoid(c0 - c1), jax.nn.sigmoid(c1 - c0)
    flat = jnp.concatenate([g0, g1, slot_ref[0:2, :]] + [jnp.zeros_like(g0)] * 4, axis=0)
    tall = jnp.transpose(flat)
    g0, g1 = tall[:, 0:1], tall[:, 1:2]
    s0, s1 = tall[:, 2:3].astype(jnp.int32), tall[:, 3:4].astype(jnp.int32)
    if peers is None:
        blocks = [(j, r_refs[0][me_ref[1] ^ j]) for j in range(4)]
    else:
        blocks = [(j, r[...]) for j, r in zip(peers, r_refs)]
    width = cap * len(blocks)
    place = lax.broadcasted_iota(jnp.int32, (tokens, width), 1)
    shift = jnp.zeros((tokens, width), jnp.int32)
    for i, (j, _) in enumerate(blocks):
        inside = (place >= i * cap) & (place < (i + 1) * cap)
        shift = jnp.where(inside, (j - i) * cap, shift)
    place = place + shift
    q0 = (place == s0).astype(F32).astype(BF)
    q1 = (place == s1).astype(F32).astype(BF)
    rows = jnp.concatenate([b for _, b in blocks], axis=0)
    total = (
        acc_ref[...].astype(F32)
        + g0 * jnp.dot(q0, rows, preferred_element_type=F32)
        + g1 * jnp.dot(q1, rows, preferred_element_type=F32)
    )
    out_ref[...] = total.astype(out_ref.dtype)


CHUNKS = ((), (0, 1, 2, 3), (4, 5), (6, 7))
ORDER = (
    ("W", 0),
    ("W", 1),
    ("X", (1,)),
    ("U", (1,), (0, 1), ((1, (0, 1)),)),
    ("W", None),
    ("U", (1,), (2, 3), ((1, (2, 3)),)),
    ("X", (2, 3)),
    ("U", (2, 3), (0, 1, 2, 3), ((3, (0, 1, 2, 3)), (2, (0, 1, 2, 3)))),
    ("H", 1, (0, 1)),
    ("H", 1, (2, 3)),
    ("D", 1, (0, 1, 2, 3)),
    ("F", 1),
    ("D", 2, (0, 1, 2, 3)),
    ("F", 2),
    ("D", 3, (0, 1, 2, 3)),
    ("F", 3),
    ("C", 1),
    ("C", 2),
    ("C", 3),
)


def pipelined(activations, router_weight, w_up, w_down, expert_ids):
    experts = router_weight.shape[0]
    tokens, columns = activations.shape
    cap = tokens // 4
    half = w_up.shape[0] // 2
    span = half // NP
    section = lax.axis_index("section").astype(jnp.int32)
    place = lax.axis_index("expert").astype(jnp.int32)
    me = jnp.stack([section % 2, place & 3])
    swap_core = [(i, i ^ 1) for i in range(4)]
    swap_y = [(i, i ^ 2) for i in range(4)]
    groups = [[0, 1, 2, 3], [4, 5, 6, 7]]

    def peer(j):
        return [(i, i ^ j) for i in range(experts)]

    def core_swap(v):
        return lax.ppermute(v, "section", swap_core)

    def core_pair(v):
        return lax.all_gather(v, "section", axis_index_groups=[[0, 1], [2, 3]])

    def near_swap(v):
        return lax.all_to_all(
            v, "expert", split_axis=0, concat_axis=0, axis_index_groups=groups, tiled=True
        )

    ids = expert_ids.T
    slots, logits, near_rows, all_rows = kernel_call(
        functools.partial(route_kernel, cap),
        out_shape=[sds((8, tokens), F32), sds((experts, tokens), F32)]
        + [sds((4, cap, columns)), sds((experts, cap, columns))],
        in_specs=[SM, VM, VM, VM],
        out_specs=[VM] * 4,
        compiler_params=params(LIMIT),
        name="route",
    )(place.reshape(1), ids, activations, router_weight)
    near = near_swap(near_rows)
    far = lax.all_to_all(all_rows, "expert", split_axis=0, concat_axis=0, tiled=True)
    mine_x, their_x = {}, {}
    tok = slots
    logits = logits + core_swap(logits)
    logits = logits + lax.ppermute(logits, "section", swap_y)
    w_up2, w_down2 = {}, None

    def cut(i):
        nonlocal tok, w_down2
        rows = half if i is None else half // 2
        tok = kernel_call(
            functools.partial(cut_kernel, i * rows if i else 0, half),
            out_shape=sds((rows, columns)),
            in_specs=[SM, HBM, ANY],
            out_specs=HBM,
            scratch_shapes=cut_scratch(rows, columns),
            compiler_params=params(LIMIT),
            name=f"cut{i}",
        )(me, w_down if i is None else w_up, tok)
        if i is None:
            w_down2 = core_swap(tok)
        else:
            w_up2[i] = core_swap(tok)

    sums, back, partial = {}, {}, {}

    def pack(chunks):
        nonlocal tok
        peers = [j for c in chunks for j in CHUNKS[c]]
        res = kernel_call(
            functools.partial(pack_kernel, cap, peers),
            out_shape=[sds((2 * cap, columns))] * 2,
            in_specs=[SM, VM, ANY],
            out_specs=[VM] * 2,
            compiler_params=params(LIMIT),
            cost_estimate=LONG if chunks == (1,) else COST,
            name=f"pack{chunks[0]}",
        )(
            (place & 3 if chunks == (1,) else place).reshape(1),
            near if chunks == (1,) else far,
            tok,
        )
        tok = res[0]
        mine_x[chunks], their_x[chunks] = res, [core_pair(r) for r in res]

    def absorb(c, pieces):
        nonlocal tok
        pair = sums[c, pieces[0]][0]
        tok = kernel_call(
            silu_kernel,
            out_shape=sds(pair[0].shape),
            in_specs=[VM, VM, ANY],
            out_specs=VM,
            compiler_params=params(LIMIT),
            cost_estimate=LONG,
            name=f"silu{c}",
        )(*pair, tok)
        for p in pieces:
            sums[c, p] = (tok, sums[c, p][1])

    def slots_of(n):
        return [
            pltpu.VMEM((min(SLOTS, n), TILE, columns), BF),
            pltpu.SemaphoreType.DMA((min(SLOTS, n),)),
        ] * 2

    def up(chunks, pieces, places):
        nonlocal tok
        n = cap * sum(len(CHUNKS[c]) for c in chunks)
        mine, theirs = mine_x[chunks], their_x[chunks]
        got = (w_up2[0], w_up2[pieces[-1] * 2 // NP])
        rows = {c: cap * sum(len(CHUNKS[d]) for d in chunks if d < c) for c in chunks}
        corners = [(rows[c], (ps[0] - pieces[0]) * span) for c, ps in places]
        outs = kernel_call(
            functools.partial(up_kernel, half, span, pieces, len(mine), corners),
            out_shape=[sds((cap * len(CHUNKS[c]), span * len(ps))) for c, ps in places],
            in_specs=[SM] + [VM] * (len(mine) + len(theirs)) + [HBM, ANY, ANY, ANY, ANY],
            out_specs=[VM] * len(places),
            scratch_shapes=[pltpu.VMEM((n, columns), BF)] * 2
            + slots_of(span * len(pieces) // TILE),
            compiler_params=params(LIMIT),
            name="up" + "".join(map(str, chunks)) + f"_{pieces[0]}",
        )(me, *mine, *theirs, w_up, *got, tok, logits)
        tok = outs[0]
        for (c, ps), out in zip(places, outs):
            pair = (out, lax.ppermute(out, "section", swap_y))
            for i, p in enumerate(ps):
                sums[c, p] = (pair, i * span)

    def down(c, pieces, final):
        nonlocal tok
        held = [p for p in pieces if not isinstance(sums[c, p][0], tuple)]
        if held and len(held) < len(pieces):
            down(c, held, False)
            pieces = [p for p in pieces if p not in held]
        ready = not isinstance(sums[c, pieces[0]][0], tuple)
        arrays, plan = [], []
        for p in pieces:
            pair, at = sums[c, p]
            if not arrays or arrays[-1] is not pair:
                arrays.append(pair)
            plan += [(p * span + t, len(arrays) - 1, at + t) for t in range(0, span, TILE)]
        flat = arrays if ready else [v for pair in arrays for v in pair]
        n = cap * len(CHUNKS[c])
        acc = partial.get(c, ())
        parts = 2 if final and c == 1 else 1
        res = kernel_call(
            functools.partial(down_kernel, half, plan, ready, len(acc) > 0),
            out_shape=[sds((n, columns), F32)] + [sds((n // parts, columns), BF if final else F32)] * parts,
            in_specs=[SM] + [VM] * len(flat) + [HBM, ANY] + [VM] * len(acc) + [ANY],
            out_specs=[VM] * (1 + parts),
            scratch_shapes=[
                pltpu.VMEM((n, TILE), BF),
                pltpu.VMEM((n, columns), F32),
                pltpu.VMEM((n, columns), F32),
            ]
            + slots_of(len(plan)),
            compiler_params=params(LIMIT),
            name=f"down{c}_{pieces[0]}",
        )(me, *flat, w_down, w_down2, *acc, tok)
        tok = res[0]
        partial[c] = (res[0], *[core_pair(r) for r in res[1:]]) if final else tuple(res)

    def finish(c):
        nonlocal tok
        own, *others = partial[c]
        peers = CHUNKS[c]
        near = c == 1
        res = kernel_call(
            functools.partial(finish_kernel, cap, near, len(others)),
            out_shape=[sds((4, cap, columns))] if near else [sds((cap, columns))] * len(peers),
            in_specs=[SM] + [VM] * (1 + len(others)) + [ANY],
            out_specs=[VM] * (1 if near else len(peers)),
            compiler_params=params(LIMIT),
            name=f"finish{c}",
        )(me, own, *others, tok)
        tok = res[0]
        if near:
            back[1] = [near_swap(res[0])]
        else:
            back[c] = [r if j == 0 else lax.ppermute(r, "expert", peer(j)) for j, r in zip(peers, res)]

    total = activations

    def combine(c, final):
        nonlocal tok, total
        total = tok = kernel_call(
            functools.partial(combine_kernel, cap, None if c == 1 else CHUNKS[c]),
            out_shape=sds((tokens, columns), BF if final else F32),
            in_specs=[SM] + [VM] * (4 + len(back[c])) + [ANY],
            out_specs=VM,
            compiler_params=params(LIMIT),
            name=f"combine{c}",
        )(me, ids, slots, logits, total, *back[c], tok)

    for i, (kind, n, *rest) in enumerate(ORDER):
        if kind == "W":
            cut(n)
        elif kind == "X":
            pack(n)
        elif kind == "U":
            up(n, *rest)
        elif kind == "H":
            absorb(n, *rest)
        elif kind == "D":
            down(n, rest[0], rest[0][-1] == NP - 1)
        elif kind == "F":
            finish(n)
        else:
            combine(n, i == len(ORDER) - 1)
    return total


def body(activations, router_weight, w_up, w_down, expert_ids):
    if (
        lax.axis_size("section") == 4
        and lax.axis_size("expert") == router_weight.shape[0] == 8
        and activations.shape[0] == 256
    ):
        return pipelined(activations, router_weight, w_up, w_down, expert_ids)
    return plain(activations, router_weight, w_up, w_down, expert_ids)


def solution(mesh):
    placed = (
        P("expert", "section"),
        P(None, "section"),
        P("expert", "section"),
        P("expert", "section"),
        P("expert", None),
    )
    return jax.shard_map(
        body, mesh=mesh, in_specs=placed, out_specs=P("expert", "section"), check_vma=False
    )
```

```python
import functools

import jax
import jax.numpy as jnp
from jax import lax
from jax.experimental import pallas as pl
from jax.experimental.pallas import tpu as pltpu
from jax.sharding import PartitionSpec as P

BF = jnp.bfloat16
F32 = jnp.float32
VM = pl.BlockSpec(memory_space=pltpu.VMEM)
ANY = pl.BlockSpec(memory_space=pl.ANY)
HBM = pl.BlockSpec(memory_space=pltpu.HBM)
LONG = pl.CostEstimate(flops=10**12, bytes_accessed=1, transcendentals=0)
COST = pl.CostEstimate(flops=1, bytes_accessed=1, transcendentals=0)
SM = pl.BlockSpec(memory_space=pltpu.SMEM)
TILE = 512
SLOTS = 4
NP = 4
LIMIT = 40


def kernel_call(kernel, **options):
    return pl.pallas_call(kernel, **{"cost_estimate": COST, **options})


def sds(shape, dtype=BF):
    return jax.ShapeDtypeStruct(shape, dtype)


def params(mib):
    return pltpu.CompilerParams(vmem_limit_bytes=mib << 20)


def plain(activations, router_weight, w_up, w_down, expert_ids):
    group = lax.axis_size("expert")
    experts = router_weight.shape[0]
    quarters = group // experts
    tok_rows, columns = activations.shape
    capacity = tok_rows // 4
    total_rows = experts * capacity
    logits = lax.psum(
        lax.dot_general(
            activations, router_weight, (((1,), (1,)), ((), ())), preferred_element_type=F32
        ),
        "section",
    )
    selected = expert_ids[:, :, None] == jnp.arange(experts, dtype=jnp.int32)[None, None, :]
    chosen = jnp.sum(jnp.where(selected, logits[:, None, :], 0.0), axis=2)
    gates = jax.nn.sigmoid(chosen - chosen[:, ::-1])
    flat_ids = expert_ids.reshape(-1)
    onehot = flat_ids[:, None] == jnp.arange(experts, dtype=jnp.int32)[None, :]
    places = jnp.arange(flat_ids.shape[0])
    before = (places[None, :] < places[:, None]).astype(BF)
    counts = jnp.dot(before, onehot.astype(BF), preferred_element_type=F32)
    rank_in = jnp.sum(jnp.where(onehot, counts, 0.0), axis=1).astype(jnp.int32)
    targets = flat_ids * capacity + rank_in
    outgoing = (
        jnp.zeros((total_rows, columns), BF).at[targets].set(jnp.repeat(activations, 2, axis=0))
    )
    outgoing = jnp.repeat(outgoing.reshape(experts, capacity, columns), quarters, axis=0)
    received = lax.all_to_all(outgoing, "expert", split_axis=0, concat_axis=0, tiled=True)
    senders, items = received.shape[:2]
    rows = received.reshape(senders * items, columns)
    pre_part = lax.dot_general(rows, w_up, (((1,), (1,)), ((), ())), preferred_element_type=F32)
    whole = lax.psum(pre_part.astype(BF), "section").astype(F32)
    hidden = jax.nn.silu(whole).astype(BF)
    result = jnp.dot(hidden, w_down, preferred_element_type=F32)
    result = result.astype(BF).reshape(senders, items, columns)
    returned = lax.all_to_all(result, "expert", split_axis=0, concat_axis=0, tiled=True)
    returned = (
        returned.reshape(experts, quarters, capacity, columns)
        .transpose(1, 0, 2, 3)
        .reshape(quarters, total_rows, columns)
    )
    onehot = (targets[:, None] == jnp.arange(total_rows)[None, :]).astype(BF)
    picked = jnp.einsum("ts,qsd->td", onehot, returned, preferred_element_type=F32)
    picked = picked.reshape(tok_rows, 2, columns)
    mixed = activations.astype(F32) + jnp.sum(gates[:, :, None] * picked, axis=1)
    return mixed.astype(BF)


PARTS = 8


def cut_copies(first, core, half, w_ref, o_ref, hold, sem):
    step = o_ref.shape[0] // PARTS
    start = pl.multiple_of((1 - core) * half + first, step)
    ins = [
        pltpu.make_async_copy(w_ref.at[pl.ds(start + i * step, step), :], hold.at[i], sem.at[i])
        for i in range(PARTS)
    ]
    outs = [
        pltpu.make_async_copy(hold.at[i], o_ref.at[pl.ds(i * step, step), :], sem.at[PARTS + i])
        for i in range(PARTS)
    ]
    return ins, outs


def pack_kernel(cap, peers, me_ref, a_ref, t_ref, *outs):
    low = me_ref[0]
    per = len(peers) // len(outs)
    for i, j in enumerate(peers):
        at = i % per * cap
        outs[i // per][at : at + cap, :] = a_ref[low ^ j]


def cut_kernel(first, half, me_ref, w_ref, t_ref, o_ref, hold, sem):
    ins, outs = cut_copies(first, me_ref[0], half, w_ref, o_ref, hold, sem)
    for c in ins:
        c.start()
    for i, o in zip(ins, outs):
        i.wait()
        o.start()
    for o in outs:
        o.wait()


def cut_scratch(rows, columns):
    return [
        pltpu.VMEM((PARTS, rows // PARTS, columns), BF),
        pltpu.SemaphoreType.DMA((2 * PARTS,)),
    ]


def route_kernel(cap, me_ref, ids_ref, act_ref, router_ref, *outs):
    slot_ref, logit_ref, near_ref, all_ref = outs
    experts = router_ref.shape[0]
    tokens = act_ref.shape[0]
    low = me_ref[0] & 3
    ids = ids_ref[...] ^ me_ref[0]
    id0, id1 = ids[0:1, :], ids[1:2, :]
    line = lax.broadcasted_iota(jnp.int32, (experts, tokens), 0)
    is0, is1 = line == id0, line == id1
    member = (is0 | is1).astype(F32).astype(BF)
    r = lax.broadcasted_iota(jnp.int32, (tokens, tokens), 0)
    c = lax.broadcasted_iota(jnp.int32, (tokens, tokens), 1)
    rank = jnp.dot(member, (r < c).astype(F32).astype(BF), preferred_element_type=F32)
    first = line.astype(F32) * cap + rank
    slot0 = jnp.sum(jnp.where(is0, first, 0.0), axis=0, keepdims=True)
    slot1 = jnp.sum(jnp.where(is1, first, 0.0), axis=0, keepdims=True)
    slot_ref[...] = jnp.concatenate([slot0, slot1] + [jnp.zeros_like(slot0)] * 6, axis=0)
    act = act_ref[...]
    i0, i1 = slot0.astype(jnp.int32), slot1.astype(jnp.int32)
    s = lax.broadcasted_iota(jnp.int32, (experts * cap, tokens), 0)
    pick = ((s == i0) | (s == i1)).astype(F32).astype(BF)
    for j in range(experts):
        rows = jnp.dot(pick[j * cap : (j + 1) * cap], act, preferred_element_type=F32).astype(BF)
        if j < 4:
            near_ref[low ^ j] = rows
        all_ref[me_ref[0] ^ j] = rows
    logit_ref[...] = lax.dot_general(
        router_ref[...], act, (((1,), (1,)), ((), ())), preferred_element_type=F32
    )


def silu_kernel(a_ref, b_ref, t_ref, o_ref):
    v = a_ref[...].astype(F32) + b_ref[...].astype(F32)
    o_ref[...] = (v / (1.0 + jnp.exp(-v))).astype(BF)


def stream(sources, count, use):
    slots = min(SLOTS, count)

    def copies(g):
        for locate, buf, sem in sources:
            ref, row = locate(g)
            yield pltpu.make_async_copy(
                ref.at[pl.ds(pl.multiple_of(row, TILE), TILE), :],
                buf.at[g % slots],
                sem.at[g % slots],
            )

    for g in range(slots):
        for c in copies(g):
            c.start()
    for g in range(count):
        for c in copies(g):
            c.wait()
        use(g, *[buf.at[g % slots] for _, buf, _ in sources])
        if g + slots < count:
            for c in copies(g + slots):
                c.start()


def up_kernel(half, span, pieces, n_x, corners, me_ref, *refs):
    mine_refs, their_refs = refs[:n_x], refs[n_x : 2 * n_x]
    w_ref, *got_refs = refs[2 * n_x : 2 * n_x + 3]
    n_p = len(pieces)
    x, y, buf_a, sem_a, buf_b, sem_b = refs[-6:]
    core = me_ref[0]
    out_refs = refs[-6 - len(corners) : -6]
    rows = mine_refs[0].shape[0]
    for i in range(n_x):
        x[i * rows : (i + 1) * rows, :] = mine_refs[i][...]
        y[i * rows : (i + 1) * rows, :] = their_refs[i][1 - core]
    each = span // TILE

    def locate_a(g):
        return w_ref, core * half + pieces[g // each] * span + (g % each) * TILE

    def locate_b(g):
        row = pieces[g // each] * span + (g % each) * TILE
        return got_refs[row // (half // 2)], row % (half // 2)

    dims = (((1,), (1,)), ((), ()))

    def use(g, a, b):
        v = (
            lax.dot_general(x[...], a[...], dims, preferred_element_type=F32)
            + lax.dot_general(y[...], b[...], dims, preferred_element_type=F32)
        ).astype(BF)
        for o, (row, col) in zip(out_refs, corners):
            at = g * TILE - col
            if 0 <= at < o.shape[1]:
                o[:, at : at + TILE] = v[row : row + o.shape[0], :]

    stream([(locate_a, buf_a, sem_a), (locate_b, buf_b, sem_b)], each * n_p, use)


def down_kernel(half, plan, n_in, has_acc, me_ref, *refs):
    s_refs = refs[:n_in]
    w_ref, got_ref = refs[n_in : n_in + 2]
    k = n_in + 2
    acc_refs = refs[k : k + 2] if has_acc else None
    k += 1 + (2 if has_acc else 0)
    own_ref, *oth_refs = refs[k:-7]
    h, own, oth, buf_a, sem_a, buf_b, sem_b = refs[-7:]
    core = me_ref[0]

    def locate_a(g):
        return w_ref, core * half + plan[g][0]

    def locate_b(g):
        return got_ref, plan[g][0]

    def use(g, a, b):
        _, which, c = plan[g]
        cols = slice(c, c + TILE)
        if len(which) == 1:
            h[...] = s_refs[which[0]][:, cols]
        else:
            v = s_refs[which[0]][:, cols].astype(F32) + s_refs[which[1]][:, cols].astype(F32)
            h[...] = (v / (1.0 + jnp.exp(-v))).astype(BF)
        for i, (total, w) in enumerate(((own, a), (oth, b))):
            part = jnp.dot(h[...], w[...], preferred_element_type=F32)
            if g == 0:
                total[...] = part + acc_refs[i][...] if has_acc else part
            else:
                total[...] += part

    stream([(locate_a, buf_a, sem_a), (locate_b, buf_b, sem_b)], len(plan), use)
    own_ref[...] = own[...]
    each = own.shape[0] // len(oth_refs)
    for i, r in enumerate(oth_refs):
        r[...] = oth[i * each : (i + 1) * each, :].astype(r.dtype)


def finish_kernel(cap, near, parts, me_ref, own_ref, *refs):
    got_refs, outs = refs[:parts], refs[parts + 1 :]
    core, low = me_ref[0], me_ref[1]
    got = jnp.concatenate([r[1 - core] for r in got_refs], axis=0)
    for i in range(own_ref.shape[0] // cap):
        rows = slice(i * cap, (i + 1) * cap)
        v = (own_ref[rows, :] + got[rows, :].astype(F32)).astype(BF)
        if near:
            outs[0][low ^ i] = v
        else:
            outs[i][...] = v


def combine_kernel(cap, peers, me_ref, ids_ref, slot_ref, logit_ref, acc_ref, *refs):
    n = 1 if peers is None else len(peers)
    r_refs = refs[:n]
    out_ref = refs[n + 1]
    experts, tokens = logit_ref.shape
    line = lax.broadcasted_iota(jnp.int32, (experts, tokens), 0)
    ids = ids_ref[...]
    logits = logit_ref[...]
    c0 = jnp.sum(jnp.where(line == ids[0:1, :], logits, 0.0), axis=0, keepdims=True)
    c1 = jnp.sum(jnp.where(line == ids[1:2, :], logits, 0.0), axis=0, keepdims=True)
    g0, g1 = jax.nn.sigmoid(c0 - c1), jax.nn.sigmoid(c1 - c0)
    flat = jnp.concatenate([g0, g1, slot_ref[0:2, :]] + [jnp.zeros_like(g0)] * 4, axis=0)
    tall = jnp.transpose(flat)
    g0, g1 = tall[:, 0:1], tall[:, 1:2]
    s0, s1 = tall[:, 2:3].astype(jnp.int32), tall[:, 3:4].astype(jnp.int32)
    if peers is None:
        blocks = [(j, r_refs[0][me_ref[1] ^ j]) for j in range(4)]
    else:
        blocks = [(j, r[...]) for j, r in zip(peers, r_refs)]
    width = cap * len(blocks)
    place = lax.broadcasted_iota(jnp.int32, (tokens, width), 1)
    shift = jnp.zeros((tokens, width), jnp.int32)
    for i, (j, _) in enumerate(blocks):
        inside = (place >= i * cap) & (place < (i + 1) * cap)
        shift = jnp.where(inside, (j - i) * cap, shift)
    place = place + shift
    q0 = (place == s0).astype(F32).astype(BF)
    q1 = (place == s1).astype(F32).astype(BF)
    rows = jnp.concatenate([b for _, b in blocks], axis=0)
    total = (
        acc_ref[...].astype(F32)
        + g0 * jnp.dot(q0, rows, preferred_element_type=F32)
        + g1 * jnp.dot(q1, rows, preferred_element_type=F32)
    )
    out_ref[...] = total.astype(out_ref.dtype)


CHUNKS = ((), (0, 1, 2, 3), (6, 7), (4, 5))
ORDER = (
    ("W", 0),
    ("W", 1),
    ("X", (1,)),
    ("U", (1,), (0, 1), ((1, (0, 1)),)),
    ("W", None),
    ("U", (1,), (2, 3), ((1, (2, 3)),)),
    ("X", (2, 3)),
    ("U", (2, 3), (0, 1, 2, 3), ((3, (0, 1, 2, 3)), (2, (0, 1, 2, 3)))),
    ("H", 1, (0, 1)),
    ("D", 1, (0, 1, 2, 3)),
    ("F", 1),
    ("D", 2, (0, 1, 2, 3)),
    ("F", 2),
    ("D", 3, (0, 1, 2, 3)),
    ("F", 3),
    ("C", 1),
    ("C", 2),
    ("C", 3),
)


def pipelined(activations, router_weight, w_up, w_down, expert_ids):
    experts = router_weight.shape[0]
    tokens, columns = activations.shape
    cap = tokens // 4
    half = w_up.shape[0] // 2
    span = half // NP
    section = lax.axis_index("section").astype(jnp.int32)
    place = lax.axis_index("expert").astype(jnp.int32)
    me = jnp.stack([section % 2, place & 3])
    swap_core = [(i, i ^ 1) for i in range(4)]
    swap_y = [(i, i ^ 2) for i in range(4)]
    groups = [[0, 1, 2, 3], [4, 5, 6, 7]]

    def peer(j):
        return [(i, i ^ j) for i in range(experts)]

    def core_swap(v):
        return lax.ppermute(v, "section", swap_core)

    def core_pair(v):
        return lax.all_gather(v, "section", axis_index_groups=[[0, 1], [2, 3]])

    def near_swap(v):
        return lax.all_to_all(
            v, "expert", split_axis=0, concat_axis=0, axis_index_groups=groups, tiled=True
        )

    ids = expert_ids.T
    slots, logits, near_rows, all_rows = kernel_call(
        functools.partial(route_kernel, cap),
        out_shape=[sds((8, tokens), F32), sds((experts, tokens), F32)]
        + [sds((4, cap, columns)), sds((experts, cap, columns))],
        in_specs=[SM, VM, VM, VM],
        out_specs=[VM] * 4,
        compiler_params=params(LIMIT),
        name="route",
    )(place.reshape(1), ids, activations, router_weight)
    near = near_swap(near_rows)
    far = lax.all_to_all(all_rows, "expert", split_axis=0, concat_axis=0, tiled=True)
    mine_x, their_x = {}, {}
    tok = slots
    logits = logits + core_swap(logits)
    logits = logits + lax.ppermute(logits, "section", swap_y)
    w_up2, w_down2 = {}, None

    def cut(i):
        nonlocal tok, w_down2
        rows = half if i is None else half // 2
        tok = kernel_call(
            functools.partial(cut_kernel, i * rows if i else 0, half),
            out_shape=sds((rows, columns)),
            in_specs=[SM, HBM, ANY],
            out_specs=HBM,
            scratch_shapes=cut_scratch(rows, columns),
            compiler_params=params(LIMIT),
            name=f"cut{i}",
        )(me, w_down if i is None else w_up, tok)
        if i is None:
            w_down2 = core_swap(tok)
        else:
            w_up2[i] = core_swap(tok)

    sums, back, partial = {}, {}, {}

    def pack(chunks):
        nonlocal tok
        peers = [j for c in chunks for j in CHUNKS[c]]
        res = kernel_call(
            functools.partial(pack_kernel, cap, peers),
            out_shape=[sds((2 * cap, columns))] * 2,
            in_specs=[SM, VM, ANY],
            out_specs=[VM] * 2,
            compiler_params=params(LIMIT),
            cost_estimate=LONG if chunks == (1,) else COST,
            name=f"pack{chunks[0]}",
        )(
            (place & 3 if chunks == (1,) else place).reshape(1),
            near if chunks == (1,) else far,
            tok,
        )
        tok = res[0]
        mine_x[chunks], their_x[chunks] = res, [core_pair(r) for r in res]

    def absorb(c, pieces):
        nonlocal tok
        pair = sums[c, pieces[0]][0]
        tok = kernel_call(
            silu_kernel,
            out_shape=sds(pair[0].shape),
            in_specs=[VM, VM, ANY],
            out_specs=VM,
            compiler_params=params(LIMIT),
            cost_estimate=LONG,
            name=f"silu{c}",
        )(*pair, tok)
        for p in pieces:
            sums[c, p] = (tok, sums[c, p][1])

    def slots_of(n):
        return [
            pltpu.VMEM((min(SLOTS, n), TILE, columns), BF),
            pltpu.SemaphoreType.DMA((min(SLOTS, n),)),
        ] * 2

    def up(chunks, pieces, places):
        nonlocal tok
        n = cap * sum(len(CHUNKS[c]) for c in chunks)
        mine, theirs = mine_x[chunks], their_x[chunks]
        got = (w_up2[0], w_up2[pieces[-1] * 2 // NP])
        rows = {c: cap * sum(len(CHUNKS[d]) for d in chunks if d < c) for c in chunks}
        corners = [(rows[c], (ps[0] - pieces[0]) * span) for c, ps in places]
        outs = kernel_call(
            functools.partial(up_kernel, half, span, pieces, len(mine), corners),
            out_shape=[sds((cap * len(CHUNKS[c]), span * len(ps))) for c, ps in places],
            in_specs=[SM] + [VM] * (len(mine) + len(theirs)) + [HBM, ANY, ANY, ANY, ANY],
            out_specs=[VM] * len(places),
            scratch_shapes=[pltpu.VMEM((n, columns), BF)] * 2
            + slots_of(span * len(pieces) // TILE),
            compiler_params=params(LIMIT),
            name="up" + "".join(map(str, chunks)) + f"_{pieces[0]}",
        )(me, *mine, *theirs, w_up, *got, tok, logits)
        tok = outs[0]
        for (c, ps), out in zip(places, outs):
            pair = (out, lax.ppermute(out, "section", swap_y))
            for i, p in enumerate(ps):
                sums[c, p] = (pair, i * span)

    def down(c, pieces, final):
        nonlocal tok
        flat, plan, last = [], [], None
        for p in pieces:
            pair, at = sums[c, p]
            if pair is not last:
                last, found = pair, pair if isinstance(pair, tuple) else (pair,)
                which = range(len(flat), len(flat) + len(found))
                flat += found
            plan += [(p * span + t, which, at + t) for t in range(0, span, TILE)]
        n = cap * len(CHUNKS[c])
        acc = partial.get(c, ())
        parts = 2 if final and c == 1 else 1
        res = kernel_call(
            functools.partial(down_kernel, half, plan, len(flat), len(acc) > 0),
            out_shape=[sds((n, columns), F32)] + [sds((n // parts, columns), BF if final else F32)] * parts,
            in_specs=[SM] + [VM] * len(flat) + [HBM, ANY] + [VM] * len(acc) + [ANY],
            out_specs=[VM] * (1 + parts),
            scratch_shapes=[
                pltpu.VMEM((n, TILE), BF),
                pltpu.VMEM((n, columns), F32),
                pltpu.VMEM((n, columns), F32),
            ]
            + slots_of(len(plan)),
            compiler_params=params(LIMIT),
            name=f"down{c}_{pieces[0]}",
        )(me, *flat, w_down, w_down2, *acc, tok)
        tok = res[0]
        partial[c] = (res[0], *[core_pair(r) for r in res[1:]]) if final else tuple(res)

    def finish(c):
        nonlocal tok
        own, *others = partial[c]
        peers = CHUNKS[c]
        near = c == 1
        res = kernel_call(
            functools.partial(finish_kernel, cap, near, len(others)),
            out_shape=[sds((4, cap, columns))] if near else [sds((cap, columns))] * len(peers),
            in_specs=[SM] + [VM] * (1 + len(others)) + [ANY],
            out_specs=[VM] * (1 if near else len(peers)),
            compiler_params=params(LIMIT),
            name=f"finish{c}",
        )(me, own, *others, tok)
        tok = res[0]
        if near:
            back[1] = [near_swap(res[0])]
        else:
            back[c] = [r if j == 0 else lax.ppermute(r, "expert", peer(j)) for j, r in zip(peers, res)]

    total = activations

    def combine(c, final):
        nonlocal tok, total
        total = tok = kernel_call(
            functools.partial(combine_kernel, cap, None if c == 1 else CHUNKS[c]),
            out_shape=sds((tokens, columns), BF if final else F32),
            in_specs=[SM] + [VM] * (4 + len(back[c])) + [ANY],
            out_specs=VM,
            compiler_params=params(LIMIT),
            name=f"combine{c}",
        )(me, ids, slots, logits, total, *back[c], tok)

    for i, (kind, n, *rest) in enumerate(ORDER):
        if kind == "W":
            cut(n)
        elif kind == "X":
            pack(n)
        elif kind == "U":
            up(n, *rest)
        elif kind == "H":
            absorb(n, *rest)
        elif kind == "D":
            down(n, rest[0], rest[0][-1] == NP - 1)
        elif kind == "F":
            finish(n)
        else:
            combine(n, i == len(ORDER) - 1)
    return total


def body(activations, router_weight, w_up, w_down, expert_ids):
    if (
        lax.axis_size("section") == 4
        and lax.axis_size("expert") == router_weight.shape[0] == 8
        and activations.shape[0] == 256
    ):
        return pipelined(activations, router_weight, w_up, w_down, expert_ids)
    return plain(activations, router_weight, w_up, w_down, expert_ids)


def solution(mesh):
    placed = (
        P("expert", "section"),
        P(None, "section"),
        P("expert", "section"),
        P("expert", "section"),
        P("expert", None),
    )
    return jax.shard_map(
        body, mesh=mesh, in_specs=placed, out_specs=P("expert", "section"), check_vma=False
    )
```
